256 devices in a mesh: seq: 32 (over z_hi, x, core), ch: 8 (over z_lo, y).
Axes of the slice: x: 4, y: 4, z: 8 (z_hi: 4, z_lo: 2; z = z_hi * 2 + z_lo), core: 2. Of those that a mesh axis runs over, the one named last changes fastest.
Arguments:
- query_act: bfloat16 [4096, 4096], P('seq', 'ch'), may hold values from -6 to 6
- key_act: bfloat16 [4096, 4096], P('seq', 'ch'), may hold values from -6 to 6
- value_act: bfloat16 [4096, 4096], P('seq', 'ch'), may hold values from -6 to 6
- filter_taps: bfloat16 [4096, 4096], P('seq', 'ch'), may hold values from -2 to 2
- out_grad: bfloat16 [4096, 4096], P('seq', 'ch'), may hold values from -6 to 6
- out_weight: bfloat16 [4096, 4096], P('ch'), may hold values from -0.09375 to 0.09375
Outputs:
- mixed_out: bfloat16 [4096, 4096], P('seq', 'ch')
- query_grad: bfloat16 [4096, 4096], P('seq', 'ch')
- key_grad: bfloat16 [4096, 4096], P('seq', 'ch')
- value_grad: bfloat16 [4096, 4096], P('seq', 'ch')
- filter_grad: float32 [4096, 4096], P('seq', 'ch')
The draws below stay inside these ranges and needn't reach their ends.
All inputs are finite; a program needn't handle non-finite values.
Results may differ from the reference program's by a relative error of at most 0.02.
Values may be sent and summed in bfloat16 or wider, within the bound.
A program may use at most 128 MiB of HBM per device.

```python
import math
import jax
import jax.numpy as jnp
from jax import lax

D = 4096
TOK_DEV = 128
TOKENS = 4096
N_SEQ = 32


def draw_filter_taps(key, part):
    generator_lineages = jax.random.split(jax.random.fold_in(key, 17), 7)
    kernel_span = TOKENS
    feature_count = D
    momentary_response = jnp.arange(kernel_span, dtype=jnp.float32)[:, None]
    slow_share = 0.5
    slow_pick = jax.random.uniform(generator_lineages[0], (feature_count,), jnp.float32) < slow_share
    slow_rate = jnp.exp(jax.random.uniform(generator_lineages[1], (feature_count,), jnp.float32, math.log(0.1 / kernel_span), math.log(2.0 / kernel_span)))
    fast_rate = jnp.exp(jax.random.uniform(generator_lineages[2], (feature_count,), jnp.float32, math.log(1.0 / 50.0), math.log(1.0 / 10.0)))
    kernel_falloff = jnp.where(slow_pick, slow_rate, fast_rate)
    kernel_magnitude = jnp.sqrt(2.0 * kernel_falloff + 1.0 / kernel_span)
    impulse_indices = jax.random.uniform(generator_lineages[3], (3,), jnp.float32, 0.0, float(kernel_span))
    impulse_keepers = jax.random.uniform(generator_lineages[4], (3,), jnp.float32, 0.5, 0.8)
    impulse_shape = jnp.prod(jnp.where(momentary_response >= impulse_indices[None, :], impulse_keepers[None, :], 1.0), axis=1, keepdims=True)
    noise_perturbation = jnp.clip(jax.random.normal(generator_lineages[6], (kernel_span, feature_count), jnp.float32), -3.0, 3.0)
    return (kernel_magnitude[None, :] * jnp.exp(-kernel_falloff[None, :] * momentary_response) * impulse_shape * noise_perturbation).astype(jnp.bfloat16)


def shard_levels(stream_key, dims, pieces, low, top_value):
    def one(position, parts):
        steps = jax.random.uniform(jax.random.fold_in(jax.random.fold_in(stream_key, 6), position), (parts,), jnp.float32, low / len(pieces), top_value / len(pieces))
        return jnp.repeat(jnp.exp(steps), dims[position] // parts).reshape((-1,) + (1,) * (len(dims) - position - 1))

    level = one(*pieces[0])
    for cut in pieces[1:]:
        level = level * one(*cut)
    return level


def noise(stream_key, extent, width, reach, shards=(), kind=jnp.bfloat16):
    result = jax.random.normal(stream_key, extent, jnp.float32) * width
    if len(shards) > 0:
        result = shard_levels(stream_key, extent, shards, -0.22, 0.18) * result
    return jnp.clip(result, min=-reach, max=reach).astype(kind)


def setup_inputs(seed: int = 0) -> dict:
    seeds = jax.random.split(jax.random.key(seed), 7)
    return {
        "query_act": noise(seeds[0], (TOKENS, D), 1.0, 6.0, ((0, 32), (1, 8))),
        "key_act": noise(seeds[1], (TOKENS, D), 1.0, 6.0, ((0, 32), (1, 8))),
        "value_act": noise(seeds[2], (TOKENS, D), 1.0, 6.0, ((0, 32), (1, 8))),
        "filter_taps": draw_filter_taps(jax.random.fold_in(seeds[6], 71), 0),
        "out_grad": noise(seeds[4], (TOKENS, D), 1.0, 6.0, ((0, 32), (1, 8))),
        "out_weight": noise(seeds[5], (D, D), D ** -0.5, 0.09375, ((0, 8),)),
    }


def dft_tables(span_rows):
    period = 2 * span_rows
    frequency = jnp.arange(span_rows, dtype=jnp.int32)
    times_in = jnp.arange(span_rows, dtype=jnp.int32)
    times_out = jnp.arange(period, dtype=jnp.int32)
    parity_in = 1.0 - 2.0 * (times_in % 2).astype(jnp.float32)
    parity_out = 1.0 - 2.0 * (times_out % 2).astype(jnp.float32)
    phase_in = ((frequency[:, None] * times_in[None, :]) % period).astype(jnp.float32) * (2.0 * math.pi / period)
    cosine_rows = jnp.cos(phase_in)
    sine_rows = jnp.where(frequency[:, None] == 0, parity_in[None, :], -jnp.sin(phase_in))
    forward_t = jnp.concatenate([cosine_rows, sine_rows], axis=0)
    phase_out = ((times_out[:, None] * frequency[None, :]) % period).astype(jnp.float32) * (2.0 * math.pi / period)
    scaling = jnp.where(frequency == 0, 1.0, 2.0).astype(jnp.float32) / period
    cosinus_table_entries = jnp.cos(phase_out) * scaling[None, :]
    sine_cols = jnp.where(frequency[None, :] == 0, parity_out[:, None] / period, -jnp.sin(phase_out) * scaling[None, :])
    inverse_t = jnp.concatenate([cosinus_table_entries, sine_cols], axis=1)
    alternate = 1.0 - 2.0 * (frequency % 2).astype(jnp.float32)
    top_sign = 1.0 - 2.0 * float(span_rows % 2)
    shift_sign = jnp.concatenate([alternate, jnp.where(frequency == 0, top_sign, alternate)])[:, None]
    pair_mask = (frequency > 0).astype(jnp.float32)[:, None]
    return forward_t, inverse_t, shift_sign, pair_mask


def split_table(forward_t):
    table_high = forward_t.astype(jnp.bfloat16)
    kept_high = lax.optimization_barrier(table_high)
    table_low = (forward_t - kept_high.astype(jnp.float32)).astype(jnp.bfloat16)
    return table_high, table_low


def packed_product(first_spec, second_spec, pair_mask, conjugate):
    half_rows = first_spec.shape[-2] // 2
    first_real = first_spec[..., :half_rows, :]
    leading_quadrature_term = first_spec[..., half_rows:, :]
    second_real = second_spec[..., :half_rows, :]
    second_imag = second_spec[..., half_rows:, :]
    cross_real = leading_quadrature_term * second_imag
    if conjugate:
        real_part = first_real * second_real + pair_mask * cross_real
        imag_part = pair_mask * (first_real * second_imag - leading_quadrature_term * second_real) + (1.0 - pair_mask) * cross_real
    else:
        real_part = first_real * second_real - pair_mask * cross_real
        imag_part = pair_mask * (first_real * second_imag + leading_quadrature_term * second_real) + (1.0 - pair_mask) * cross_real
    return jnp.concatenate([real_part, imag_part], axis=-2)


def spectral_sums(spec_u, spec_h, spec_g, own_index, shift_sign, pair_mask):
    block_count = spec_u.shape[0]
    float_u = spec_u.astype(jnp.float32)
    float_h = spec_h.astype(jnp.float32)
    float_g = spec_g.astype(jnp.float32)
    empty = jnp.zeros((1,) + float_u.shape[1:], jnp.float32)
    padding = jnp.zeros(float_u.shape, jnp.float32)
    shifted_u = jnp.concatenate([empty, float_u[:-1]], axis=0) + shift_sign * float_u
    ahead_g = float_g + shift_sign * jnp.concatenate([float_g[1:], empty], axis=0)
    reversed_h = jnp.concatenate([float_h[::-1], padding], axis=0)
    ahead_ext = jnp.concatenate([ahead_g, padding], axis=0)
    chosen_h = lax.dynamic_slice_in_dim(reversed_h, (block_count - 1 - own_index).astype(jnp.int32), block_count, 0)
    chosen_g = lax.dynamic_slice_in_dim(ahead_ext, own_index.astype(jnp.int32), block_count, 0)
    conv_spec = jnp.sum(packed_product(shifted_u, chosen_h, pair_mask, False), axis=0)
    ugrad_spec = jnp.sum(packed_product(float_h, chosen_g, pair_mask, True), axis=0)
    hgrad_spec = jnp.sum(packed_product(float_u, chosen_g, pair_mask, True), axis=0)
    return conv_spec, ugrad_spec, hgrad_spec


def reference(query_act, key_act, value_act, filter_taps, out_grad, out_weight):
    span_rows = TOK_DEV
    block_count = N_SEQ
    feature_count = D
    total_rows = span_rows * block_count
    forward_t, inverse_t, shift_sign, pair_mask = dft_tables(span_rows)
    table_high, table_low = split_table(forward_t)

    def spectra_of(series):
        blocks = series.reshape(block_count, span_rows, feature_count).astype(jnp.float32)
        high_part = jnp.einsum("pt,ntc->npc", table_high.astype(jnp.float32), blocks, precision=lax.Precision.HIGHEST)
        low_part = jnp.einsum("pt,ntc->npc", table_low.astype(jnp.float32), blocks, precision=lax.Precision.HIGHEST)
        return (high_part + low_part).astype(jnp.bfloat16)

    product = (key_act.astype(jnp.float32) * value_act.astype(jnp.float32)).astype(jnp.bfloat16)
    spec_u = spectra_of(product)
    spec_h = spectra_of(filter_taps)
    gated_grad = jnp.dot(out_grad, out_weight.T, preferred_element_type=jnp.float32)
    conv_grad = (gated_grad * query_act.astype(jnp.float32)).astype(jnp.bfloat16)
    spec_g = spectra_of(conv_grad)

    def per_block(own_index):
        return spectral_sums(spec_u, spec_h, spec_g, own_index, shift_sign, pair_mask)

    conv_specs, ugrad_specs, hgrad_specs = lax.map(per_block, jnp.arange(block_count, dtype=jnp.int32))
    conv = jnp.einsum("tp,npc->ntc", inverse_t[span_rows:], conv_specs, precision=lax.Precision.HIGHEST).reshape(total_rows, feature_count)
    u_grad = jnp.einsum("tp,npc->ntc", inverse_t[:span_rows], ugrad_specs, precision=lax.Precision.HIGHEST).reshape(total_rows, feature_count)
    filter_grad = jnp.einsum("tp,npc->ntc", inverse_t[:span_rows], hgrad_specs, precision=lax.Precision.HIGHEST).reshape(total_rows, feature_count)
    gated = (query_act.astype(jnp.float32) * conv).astype(jnp.bfloat16)
    mixed_out = jnp.dot(gated, out_weight, preferred_element_type=jnp.float32).astype(jnp.bfloat16)
    query_grad = (gated_grad * conv).astype(jnp.bfloat16)
    key_grad = (u_grad * value_act.astype(jnp.float32)).astype(jnp.bfloat16)
    value_grad = (u_grad * key_act.astype(jnp.float32)).astype(jnp.bfloat16)
    return (mixed_out, query_grad, key_grad, value_grad, filter_grad)
```

```python
import functools
import math

import jax
import jax.numpy as jnp
import numpy as np
from jax import lax
from jax.experimental import pallas as pl
from jax.experimental.pallas import tpu as pltpu
from jax.sharding import PartitionSpec as P

MESH = pl.DeviceIdType.MESH
F32 = jnp.float32
BF16 = jnp.bfloat16


def transform_tables(block_count, span_rows, own_channels):
    blocks = np.arange(block_count)
    times = np.arange(span_rows)
    across = 2.0 * math.pi * np.outer(2 * blocks + 1, blocks) / (4 * block_count)
    turn = 2.0 * math.pi * np.outer(2 * blocks + 1, times) / (4 * block_count * span_rows)
    within = 2.0 * math.pi * (np.outer(times, times) % span_rows) / span_rows
    each = np.eye(own_channels)
    across_fwd = np.concatenate([np.kron(np.cos(across), each), np.kron(-np.sin(across), each)], axis=0)
    across_inv = across_fwd.T / (block_count * span_rows)
    within_fwd = np.block([[np.cos(within), -np.sin(within)], [np.sin(within), np.cos(within)]])
    turn_cos = np.repeat(np.cos(turn), own_channels, axis=0)
    turn_sin = np.repeat(np.sin(turn), own_channels, axis=0)
    return (
        jnp.asarray(across_fwd, BF16),
        jnp.asarray(across_inv, BF16),
        jnp.asarray(within_fwd, BF16),
        jnp.asarray(within_fwd.T, BF16),
        jnp.asarray(turn_cos, F32),
        jnp.asarray(turn_sin, F32),
    )


def layer_kernel(
    n_seq,
    n_ch,
    q_ref,
    k_ref,
    v_ref,
    h_ref,
    og_ref,
    w_hbm,
    kf_hbm,
    ki_hbm,
    df_hbm,
    di_hbm,
    tc_hbm,
    ts_hbm,
    mixed_ref,
    qg_ref,
    kg_ref,
    vg_ref,
    fg_ref,
    w,
    kf,
    ki,
    df,
    di,
    tc,
    ts,
    uh_src,
    uh,
    cv_src,
    cv,
    g_src,
    g,
    dd_src,
    dd,
    og,
    rs_src,
    rs,
    level,
    spec_uh,
    spec_out,
    turned,
    gg,
    own_part,
    load_sem,
    send_sem,
    recv_sem,
    ag_send,
    ag_recv,
    rs_send,
    rs_recv,
):
    seq = lax.axis_index("seq")
    ch = lax.axis_index("ch")
    rows, width = q_ref.shape
    lanes = rows
    half = n_seq * (width // n_seq)
    part = width
    step_rows = min(128, half)

    loads = [
        pltpu.make_async_copy(src, dst, load_sem.at[i])
        for i, (src, dst) in enumerate(
            [(kf_hbm, kf), (ki_hbm, ki), (df_hbm, df), (di_hbm, di), (tc_hbm, tc), (ts_hbm, ts), (w_hbm, w)]
        )
    ]
    for load in loads:
        load.start()

    barrier = pltpu.get_barrier_semaphore()

    def greet_seq(i, carry):
        pl.semaphore_signal(
            barrier, inc=1, device_id={"seq": lax.rem(seq + i, n_seq)}, device_id_type=MESH
        )
        return carry

    def greet_ch(i, carry):
        pl.semaphore_signal(
            barrier, inc=1, device_id={"ch": lax.rem(ch + i, n_ch)}, device_id_type=MESH
        )
        return carry

    lax.fori_loop(1, n_seq, greet_seq, 0)
    lax.fori_loop(1, n_ch, greet_ch, 0)

    u = (k_ref[...].astype(F32) * v_ref[...].astype(F32)).astype(BF16)
    uh_src[:, :, :lanes] = u.T.reshape(n_seq, width // n_seq, rows)
    uh_src[:, :, lanes:] = h_ref[...].T.reshape(n_seq, width // n_seq, rows)

    pl.semaphore_wait(barrier, n_seq + n_ch - 2)

    def exchange(src, dst, slot):
        def one(i, carry):
            peer = lax.rem(seq + i, n_seq)
            pltpu.make_async_remote_copy(
                src_ref=src.at[peer],
                dst_ref=dst.at[seq],
                send_sem=send_sem.at[slot],
                recv_sem=recv_sem.at[slot],
                device_id={"seq": peer},
                device_id_type=MESH,
            ).start()
            return carry

        lax.fori_loop(1, n_seq, one, 0)
        dst[seq] = src[seq]

    def arrived(dst, slot):
        landed = dst.at[pl.ds(0, n_seq - 1)]
        pltpu.make_async_copy(landed, landed, recv_sem.at[slot]).wait()

    def departed(src, slot):
        left = src.at[pl.ds(0, n_seq - 1)]
        pltpu.make_async_copy(left, left, send_sem.at[slot]).wait()

    def gather_copy(d):
        peer = lax.rem(ch + d, n_ch)
        return pltpu.make_async_remote_copy(
            src_ref=og_ref,
            dst_ref=og.at[ch],
            send_sem=ag_send.at[d],
            recv_sem=ag_recv.at[d],
            device_id={"ch": peer},
            device_id_type=MESH,
        )

    exchange(uh_src, uh, 0)
    for d in range(1, n_ch):
        gather_copy(d).start()

    for load in loads[:-1]:
        load.wait()

    def forward(values, count, put):
        level[:, : count * lanes] = jnp.dot(kf[...], values, preferred_element_type=F32)
        for r in range(0, half, step_rows):
            c, s = tc[r : r + step_rows, :], ts[r : r + step_rows, :]
            for a in range(count):
                re = level[r : r + step_rows, a * lanes : (a + 1) * lanes]
                im = level[half + r : half + r + step_rows, a * lanes : (a + 1) * lanes]
                z = jnp.concatenate([re * c + im * s, im * c - re * s], axis=1).astype(BF16)
                put(r, a, jnp.dot(z, df[...], preferred_element_type=F32))

    def inverse(product, count, dst):
        for r in range(0, half, step_rows):
            c, s = tc[r : r + step_rows, :], ts[r : r + step_rows, :]
            for a in range(count):
                x = jnp.dot(product(r, a), di[...], preferred_element_type=F32)
                re, im = x[:, :lanes], x[:, lanes:]
                turned[r : r + step_rows, a * lanes : (a + 1) * lanes] = (re * c - im * s).astype(BF16)
                turned[half + r : half + r + step_rows, a * lanes : (a + 1) * lanes] = (
                    im * c + re * s
                ).astype(BF16)
        y = jnp.dot(ki[...], turned[:, : count * lanes], preferred_element_type=F32)
        dst[...] = y.astype(BF16).reshape(dst.shape)

    def put_uh(r, a, value):
        spec_uh[a, r : r + step_rows, :] = value

    def conv_product(r, a):
        x, y = spec_uh[0, r : r + step_rows, :], spec_uh[1, r : r + step_rows, :]
        xr, xi, yr, yi = x[:, :lanes], x[:, lanes:], y[:, :lanes], y[:, lanes:]
        return jnp.concatenate([xr * yr - xi * yi, xr * yi + xi * yr], axis=1).astype(BF16)

    arrived(uh, 0)
    forward(uh[...].reshape(half, 2 * lanes), 2, put_uh)
    inverse(conv_product, 1, cv_src)
    exchange(cv_src, cv, 1)

    loads[-1].wait()

    def grad_block(value, source):
        columns = pl.ds(pl.multiple_of(source * part, part), part)
        return lax.dot_general(value, w[:, columns], (((1,), (1,)), ((), ())), preferred_element_type=F32)

    gg[...] = grad_block(og_ref[...], ch)
    for d in range(1, n_ch):
        gather_copy(d).wait_recv()
        source = lax.rem(ch + n_ch - d, n_ch)
        gg[...] += grad_block(og[source], source)
    conv_grad = (gg[...] * q_ref[...].astype(F32)).astype(BF16)
    g_src[...] = conv_grad.T.reshape(g_src.shape)
    exchange(g_src, g, 2)

    arrived(cv, 1)
    conv = cv[...].reshape(width, rows).T.astype(F32)
    qg_ref[...] = (gg[...] * conv).astype(BF16)
    gated = (q_ref[...].astype(F32) * conv).astype(BF16)

    def scatter_copy(d):
        peer = lax.rem(ch + d, n_ch)
        return pltpu.make_async_remote_copy(
            src_ref=rs_src.at[d],
            dst_ref=rs.at[d],
            send_sem=rs_send.at[d],
            recv_sem=rs_recv.at[d],
            device_id={"ch": peer},
            device_id_type=MESH,
        )

    def out_block(target):
        columns = pl.ds(pl.multiple_of(target * part, part), part)
        return jnp.dot(gated, w[:, columns], preferred_element_type=F32)

    for d in range(1, n_ch):
        rs_src[d] = out_block(lax.rem(ch + d, n_ch)).astype(BF16)
        scatter_copy(d).start()
    own_part[...] = out_block(ch)

    def put_g(r, a, value):
        gr, gi = value[:, :lanes], value[:, lanes:]
        for b in range(2):
            x = spec_uh[1 - b, r : r + step_rows, :]
            xr, xi = x[:, :lanes], x[:, lanes:]
            spec_out[b, r : r + step_rows, :] = jnp.concatenate(
                [xr * gr + xi * gi, xr * gi - xi * gr], axis=1
            ).astype(BF16)

    arrived(g, 2)
    forward(g[...].reshape(half, lanes), 1, put_g)
    inverse(lambda r, a: spec_out[a, r : r + step_rows, :], 2, dd_src)
    exchange(dd_src, dd, 3)

    total = own_part[...]
    for d in range(1, n_ch):
        scatter_copy(d).wait_recv()
        total = total + rs[d].astype(F32)
    mixed_ref[...] = total.astype(BF16)

    arrived(dd, 3)
    u_grad = dd[:, :, :lanes].reshape(width, rows).T.astype(F32)
    kg_ref[...] = (u_grad * v_ref[...].astype(F32)).astype(BF16)
    vg_ref[...] = (u_grad * k_ref[...].astype(F32)).astype(BF16)
    fg_ref[...] = dd[:, :, lanes:].reshape(width, rows).T.astype(F32)

    departed(uh_src, 0)
    departed(cv_src, 1)
    departed(g_src, 2)
    departed(dd_src, 3)
    for d in range(1, n_ch):
        gather_copy(d).wait_send()
        scatter_copy(d).wait_send()


def per_device(query_act, key_act, value_act, filter_taps, out_grad, out_weight):
    rows, width = query_act.shape
    n_seq, n_ch = lax.axis_size("seq"), lax.axis_size("ch")
    own = width // n_seq
    tables = transform_tables(n_seq, rows, own)
    half = n_seq * own
    vmem, anywhere = pl.BlockSpec(memory_space=pltpu.VMEM), pl.BlockSpec(memory_space=pl.ANY)
    bf = jax.ShapeDtypeStruct((rows, width), BF16)

    def blocks(lanes):
        return pltpu.VMEM((n_seq, own, lanes), BF16)

    return pl.pallas_call(
        functools.partial(layer_kernel, n_seq, n_ch),
        out_shape=(bf, bf, bf, bf, jax.ShapeDtypeStruct((rows, width), F32)),
        in_specs=[vmem] * 5 + [anywhere] * 7,
        out_specs=(vmem,) * 5,
        scratch_shapes=[
            pltpu.VMEM(out_weight.shape, BF16),
            *[pltpu.VMEM(t.shape, t.dtype) for t in tables],
            blocks(2 * rows),
            blocks(2 * rows),
            blocks(rows),
            blocks(rows),
            blocks(rows),
            blocks(rows),
            blocks(2 * rows),
            blocks(2 * rows),
            pltpu.VMEM((n_ch, rows, width), BF16),
            pltpu.VMEM((n_ch, rows, width), BF16),
            pltpu.VMEM((n_ch, rows, width), BF16),
            pltpu.VMEM((2 * half, 2 * rows), F32),
            pltpu.VMEM((2, half, 2 * rows), F32),
            pltpu.VMEM((2, half, 2 * rows), BF16),
            pltpu.VMEM((2 * half, 2 * rows), BF16),
            pltpu.VMEM((rows, width), F32),
            pltpu.VMEM((rows, width), F32),
            pltpu.SemaphoreType.DMA((7,)),
            pltpu.SemaphoreType.DMA((4,)),
            pltpu.SemaphoreType.DMA((4,)),
            pltpu.SemaphoreType.DMA((n_ch,)),
            pltpu.SemaphoreType.DMA((n_ch,)),
            pltpu.SemaphoreType.DMA((n_ch,)),
            pltpu.SemaphoreType.DMA((n_ch,)),
        ],
        compiler_params=pltpu.CompilerParams(
            collective_id=0, has_side_effects=True, vmem_limit_bytes=48 * 1024 * 1024
        ),
    )(query_act, key_act, value_act, filter_taps, out_grad, out_weight, *tables)


def solution(mesh):
    return jax.shard_map(
        per_device,
        mesh=mesh,
        in_specs=(P("seq", "ch"),) * 5 + (P("ch", None),),
        out_specs=(P("seq", "ch"),) * 5,
        check_vma=False,
    )
```

```python
import functools
import math

import jax
import jax.numpy as jnp
import numpy as np
from jax import lax
from jax.experimental import pallas as pl
from jax.experimental.pallas import tpu as pltpu
from jax.sharding import PartitionSpec as P

MESH = pl.DeviceIdType.MESH
F32 = jnp.float32
BF16 = jnp.bfloat16


NEAR = ((0, 1), (0, -1))
GATHER_ROUTES = ((1, 0), (0, 2)) + NEAR + NEAR + ((1, 0),)
GATHER_BLOCKS = ((0, 0),) * 4 + ((1, 0), (1, 0), (0, 2))
GATHER_PASSED = ((0, (4, 5)), (1, (6,)))
GATHER_SOURCES = ((1, 0), (0, 2), (0, -1), (0, 1), (1, -1), (1, 1), (1, 2))
GATHER_ORDER = (0, 1, 2, 3, 4, 5, 6)
SCATTER_ROUTES = ((1, 0),) + NEAR + NEAR + ((0, 2), (1, 0))
SCATTER_BLOCKS = ((1, 2), (1, 1), (1, -1), (0, 1), (0, -1), (0, 2), (1, 0))
SCATTER_ADDS = ((), (), (), (), (), (0,), (1, 2))
GREETED = ((1, 0), (0, 2)) + NEAR


def peers_far_first(seq, n_seq):
    if n_seq < 32:
        return [(seq + i) % n_seq for i in range(1, n_seq)]
    z_now, x_now, core_now = seq // 8, seq // 2 % 4, seq % 2
    z = [(z_now + d) % 4 * 8 for d in range(4)]
    x = [(x_now + d) % 4 * 2 for d in range(4)]
    core = [core_now, 1 - core_now]
    hops = sorted(
        (-(2 * min(dz, 4 - dz) + min(dx, 4 - dx)), -dc, dz, dx)
        for dz in range(4)
        for dx in range(4)
        for dc in range(2)
        if dz or dx or dc
    )
    return [z[dz] + x[dx] + core[-dc] for _, dc, dz, dx in hops]


def transform_tables(block_count, span_rows, own_channels):
    blocks = np.arange(block_count)
    times = np.arange(span_rows)
    across = 2.0 * math.pi * np.outer(2 * blocks + 1, blocks) / (4 * block_count)
    turn = 2.0 * math.pi * np.outer(2 * blocks + 1, times) / (4 * block_count * span_rows)
    within = 2.0 * math.pi * (np.outer(times, times) % span_rows) / span_rows
    each = np.eye(own_channels)
    across_fwd = np.concatenate([np.kron(np.cos(across), each), np.kron(-np.sin(across), each)], axis=0)
    across_inv = across_fwd.T / (block_count * span_rows)
    within_fwd = np.block([[np.cos(within), -np.sin(within)], [np.sin(within), np.cos(within)]])
    turn_cos = np.repeat(np.cos(turn), own_channels, axis=0)
    turn_sin = np.repeat(np.sin(turn), own_channels, axis=0)
    return (
        jnp.asarray(across_fwd, BF16),
        jnp.asarray(across_inv, BF16),
        jnp.asarray(within_fwd, BF16),
        jnp.asarray(within_fwd.T, BF16),
        jnp.asarray(turn_cos, F32),
        jnp.asarray(turn_sin, F32),
    )


def layer_kernel(
    n_seq,
    n_ch,
    q_hbm,
    k_hbm,
    v_hbm,
    h_hbm,
    og_hbm,
    w_hbm,
    kf_hbm,
    ki_hbm,
    df_hbm,
    di_hbm,
    tc_hbm,
    ts_hbm,
    mixed_ref,
    qg_ref,
    dd,
    q_ref,
    k_ref,
    v_ref,
    h_ref,
    og_ref,
    w,
    kf,
    ki,
    df,
    di,
    tc,
    ts,
    uh_src,
    uh,
    cv_src,
    cv,
    g_src,
    g,
    dd_src,
    og,
    rs_src,
    rs,
    level,
    spec_uh,
    spec_out,
    turned,
    gg,
    load_sem,
    send_sem,
    recv_sem,
    ag_send,
    ag_recv,
    rs_send,
    rs_recv,
):
    seq = lax.axis_index("seq")
    ch = lax.axis_index("ch")
    rows, width = q_hbm.shape
    lanes = rows
    half = n_seq * (width // n_seq)
    part = width
    step_rows = min(128, half)
    n_y = n_ch // 2
    plane, row = ch // n_y, ch % n_y

    def column(d_plane, d_row):
        return ((plane + d_plane) % 2) * n_y + (row + d_row) % n_y

    far_first = peers_far_first(seq, n_seq)

    loads = [
        pltpu.make_async_copy(src, dst, load_sem.at[i])
        for i, (src, dst) in enumerate(
            [
                (k_hbm, k_ref),
                (v_hbm, v_ref),
                (h_hbm, h_ref),
                (og_hbm, og_ref),
                (kf_hbm, kf),
                (tc_hbm, tc),
                (ts_hbm, ts),
                (df_hbm, df),
                (di_hbm, di),
                (ki_hbm, ki),
                (w_hbm, w),
                (q_hbm, q_ref),
            ]
        )
    ]
    for load in loads:
        load.start()

    barrier = pltpu.get_barrier_semaphore()

    with jax.named_scope("greet"):
        for peer in far_first:
            pl.semaphore_signal(barrier, inc=1, device_id={"seq": peer}, device_id_type=MESH)
        for d_plane, d_row in GREETED:
            pl.semaphore_signal(
                barrier, inc=1, device_id={"ch": column(d_plane, d_row)}, device_id_type=MESH
            )

    with jax.named_scope("product"):
        for load in loads[:3]:
            load.wait()
        u = (k_ref[...].astype(F32) * v_ref[...].astype(F32)).astype(BF16)
        uh_src[:, :, :lanes] = u.T.reshape(n_seq, width // n_seq, rows)
        uh_src[:, :, lanes:] = h_ref[...].T.reshape(n_seq, width // n_seq, rows)

    with jax.named_scope("barrier"):
        pl.semaphore_wait(barrier, n_seq - 1 + len(GREETED))

    def exchange(src, dst, slot):
        for peer in far_first:
            pltpu.make_async_remote_copy(
                src_ref=src.at[peer],
                dst_ref=dst.at[seq],
                send_sem=send_sem.at[slot],
                recv_sem=recv_sem.at[slot],
                device_id={"seq": peer},
                device_id_type=MESH,
            ).start()
        dst[seq] = src[seq]

    def arrived(dst, slot):
        landed = dst.at[pl.ds(0, n_seq - 1)]
        pltpu.make_async_copy(landed, landed, recv_sem.at[slot]).wait()

    def departed(src, slot):
        left = src.at[pl.ds(0, n_seq - 1)]
        pltpu.make_async_copy(left, left, send_sem.at[slot]).wait()

    def gather_copy(kind):
        moved = GATHER_BLOCKS[kind]
        block = column(*moved)
        return pltpu.make_async_remote_copy(
            src_ref=og_ref if moved == (0, 0) else og.at[block],
            dst_ref=og.at[block],
            send_sem=ag_send.at[kind],
            recv_sem=ag_recv.at[kind],
            device_id={"ch": column(*GATHER_ROUTES[kind])},
            device_id_type=MESH,
        )

    with jax.named_scope("send_uh_og"):
        exchange(uh_src, uh, 0)
        loads[3].wait()
        for kind in range(4):
            gather_copy(kind).start()
        for load in loads[4:10]:
            load.wait()
    with jax.named_scope("pass_on_og"):
        for needed, kinds in GATHER_PASSED:
            gather_copy(needed).wait_recv()
            for kind in kinds:
                gather_copy(kind).start()

    def forward(values, count, put):
        level[:, : count * lanes] = jnp.dot(kf[...], values, preferred_element_type=F32)
        for r in range(0, half, step_rows):
            c, s = tc[r : r + step_rows, :], ts[r : r + step_rows, :]
            for a in range(count):
                re = level[r : r + step_rows, a * lanes : (a + 1) * lanes]
                im = level[half + r : half + r + step_rows, a * lanes : (a + 1) * lanes]
                z = jnp.concatenate([re * c + im * s, im * c - re * s], axis=1).astype(BF16)
                put(r, a, jnp.dot(z, df[...], preferred_element_type=F32))

    def inverse(product, count, dst):
        for r in range(0, half, step_rows):
            c, s = tc[r : r + step_rows, :], ts[r : r + step_rows, :]
            for a in range(count):
                x = jnp.dot(product(r, a), di[...], preferred_element_type=F32)
                re, im = x[:, :lanes], x[:, lanes:]
                turned[r : r + step_rows, a * lanes : (a + 1) * lanes] = (re * c - im * s).astype(BF16)
                turned[half + r : half + r + step_rows, a * lanes : (a + 1) * lanes] = (
                    im * c + re * s
                ).astype(BF16)
        y = jnp.dot(ki[...], turned[:, : count * lanes], preferred_element_type=F32)
        dst[...] = y.astype(BF16).reshape(dst.shape)

    def put_uh(r, a, value):
        spec_uh[a, r : r + step_rows, :] = value

    def conv_product(r, a):
        x, y = spec_uh[0, r : r + step_rows, :], spec_uh[1, r : r + step_rows, :]
        xr, xi, yr, yi = x[:, :lanes], x[:, lanes:], y[:, :lanes], y[:, lanes:]
        return jnp.concatenate([xr * yr - xi * yi, xr * yi + xi * yr], axis=1).astype(BF16)

    with jax.named_scope("wait_uh"):
        arrived(uh, 0)
    with jax.named_scope("forward_uh"):
        forward(uh[...].reshape(half, 2 * lanes), 2, put_uh)
    with jax.named_scope("inverse_conv"):
        inverse(conv_product, 1, cv_src)
    with jax.named_scope("send_conv"):
        exchange(cv_src, cv, 1)

    loads[10].wait()
    loads[11].wait()

    def grad_block(value, source):
        columns = pl.ds(pl.multiple_of(source * part, part), part)
        return lax.dot_general(value, w[:, columns], (((1,), (1,)), ((), ())), preferred_element_type=F32)

    with jax.named_scope("gate_grad"):
        gg[...] = grad_block(og_ref[...], ch)
        for kind in GATHER_ORDER:
            if kind >= len(GATHER_PASSED):
                gather_copy(kind).wait_recv()
            source = column(*GATHER_SOURCES[kind])
            gg[...] += grad_block(og[source], source)
    with jax.named_scope("send_g"):
        conv_grad = (gg[...] * q_ref[...].astype(F32)).astype(BF16)
        g_src[...] = conv_grad.T.reshape(g_src.shape)
        exchange(g_src, g, 2)

    with jax.named_scope("wait_conv"):
        arrived(cv, 1)
    with jax.named_scope("gate"):
        conv = cv[...].reshape(width, rows).T.astype(F32)
        qg_ref[...] = (gg[...] * conv).astype(BF16)
        gated = (q_ref[...].astype(F32) * conv).astype(BF16)

    def scatter_copy(kind):
        return pltpu.make_async_remote_copy(
            src_ref=rs_src.at[kind],
            dst_ref=rs.at[kind],
            send_sem=rs_send.at[kind],
            recv_sem=rs_recv.at[kind],
            device_id={"ch": column(*SCATTER_ROUTES[kind])},
            device_id_type=MESH,
        )

    def out_block(target):
        columns = pl.ds(pl.multiple_of(target * part, part), part)
        return jnp.dot(gated, w[:, columns], preferred_element_type=F32)

    def send_block(kind):
        total = out_block(column(*SCATTER_BLOCKS[kind]))
        for earlier in SCATTER_ADDS[kind]:
            scatter_copy(earlier).wait_recv()
            total = total + rs[earlier].astype(F32)
        rs_src[kind] = total.astype(BF16)
        scatter_copy(kind).start()

    with jax.named_scope("out_blocks"):
        for kind in range(5):
            send_block(kind)

    def put_g(r, a, value):
        gr, gi = value[:, :lanes], value[:, lanes:]
        for b in range(2):
            x = spec_uh[1 - b, r : r + step_rows, :]
            xr, xi = x[:, :lanes], x[:, lanes:]
            spec_out[b, r : r + step_rows, :] = jnp.concatenate(
                [xr * gr + xi * gi, xr * gi - xi * gr], axis=1
            ).astype(BF16)

    with jax.named_scope("wait_g"):
        arrived(g, 2)
    with jax.named_scope("forward_g"):
        forward(g[...].reshape(half, lanes), 1, put_g)
    with jax.named_scope("inverse_grads"):
        inverse(lambda r, a: spec_out[a, r : r + step_rows, :], 2, dd_src)
    with jax.named_scope("send_grads"):
        exchange(dd_src, dd, 3)

    with jax.named_scope("mixed_sum"):
        send_block(5)
        send_block(6)
        total = out_block(ch)
        for kind in range(3, 7):
            scatter_copy(kind).wait_recv()
            total = total + rs[kind].astype(F32)
        mixed_ref[...] = total.astype(BF16)

    with jax.named_scope("wait_grads"):
        arrived(dd, 3)
    with jax.named_scope("departures"):
        departed(uh_src, 0)
        departed(cv_src, 1)
        departed(g_src, 2)
        departed(dd_src, 3)
        for kind in range(7):
            gather_copy(kind).wait_send()
            scatter_copy(kind).wait_send()


def finish_kernel(
    mixed_in, qg_in, dd, k_hbm, v_hbm, mixed_out, qg_out, kg_out, vg_out, fg_out, k_ref, v_ref, kg, vg, fg, sem
):
    n_seq, own, lanes = dd.shape
    rows, width = k_ref.shape
    lanes = lanes // 2
    first = [
        pltpu.make_async_copy(src, dst, sem.at[i])
        for i, (src, dst) in enumerate([(k_hbm, k_ref), (v_hbm, v_ref), (mixed_in, mixed_out), (qg_in, qg_out)])
    ]
    last = [
        pltpu.make_async_copy(src, dst, sem.at[4 + i])
        for i, (src, dst) in enumerate([(fg, fg_out), (kg, kg_out), (vg, vg_out)])
    ]
    for copy in first:
        copy.start()
    fg[...] = dd[:, :, lanes:].reshape(width, rows).T.astype(F32)
    last[0].start()
    u_grad = dd[:, :, :lanes].reshape(width, rows).T.astype(F32)
    first[0].wait()
    first[1].wait()
    kg[...] = (u_grad * v_ref[...].astype(F32)).astype(BF16)
    last[1].start()
    vg[...] = (u_grad * k_ref[...].astype(F32)).astype(BF16)
    last[2].start()
    for copy in first[2:] + last:
        copy.wait()


def per_device(query_act, key_act, value_act, filter_taps, out_grad, out_weight):
    rows, width = query_act.shape
    n_seq, n_ch = lax.axis_size("seq"), lax.axis_size("ch")
    own = width // n_seq
    tables = transform_tables(n_seq, rows, own)
    half = n_seq * own
    vmem, anywhere = pl.BlockSpec(memory_space=pltpu.VMEM), pl.BlockSpec(memory_space=pl.ANY)
    bf = jax.ShapeDtypeStruct((rows, width), BF16)

    def blocks(lanes):
        return pltpu.VMEM((n_seq, own, lanes), BF16)

    full = pltpu.VMEM((rows, width), BF16)
    mixed, query_grad, sums = pl.pallas_call(
        functools.partial(layer_kernel, n_seq, n_ch),
        out_shape=(bf, bf, jax.ShapeDtypeStruct((n_seq, own, 2 * rows), BF16)),
        in_specs=[anywhere] * 12,
        out_specs=(vmem,) * 3,
        scratch_shapes=[
            full,
            full,
            full,
            full,
            full,
            pltpu.VMEM(out_weight.shape, BF16),
            *[pltpu.VMEM(t.shape, t.dtype) for t in tables],
            blocks(2 * rows),
            blocks(2 * rows),
            blocks(rows),
            blocks(rows),
            blocks(rows),
            blocks(rows),
            blocks(2 * rows),
            pltpu.VMEM((n_ch, rows, width), BF16),
            pltpu.VMEM((7, rows, width), BF16),
            pltpu.VMEM((7, rows, width), BF16),
            pltpu.VMEM((2 * half, 2 * rows), F32),
            pltpu.VMEM((2, half, 2 * rows), F32),
            pltpu.VMEM((2, half, 2 * rows), BF16),
            pltpu.VMEM((2 * half, 2 * rows), BF16),
            pltpu.VMEM((rows, width), F32),
            pltpu.SemaphoreType.DMA((12,)),
            pltpu.SemaphoreType.DMA((4,)),
            pltpu.SemaphoreType.DMA((4,)),
            pltpu.SemaphoreType.DMA((7,)),
            pltpu.SemaphoreType.DMA((7,)),
            pltpu.SemaphoreType.DMA((7,)),
            pltpu.SemaphoreType.DMA((7,)),
        ],
        compiler_params=pltpu.CompilerParams(
            collective_id=0, has_side_effects=True, vmem_limit_bytes=60 * 1024 * 1024
        ),
    )(query_act, key_act, value_act, filter_taps, out_grad, out_weight, *tables)
    return pl.pallas_call(
        finish_kernel,
        out_shape=(bf, bf, bf, bf, jax.ShapeDtypeStruct((rows, width), F32)),
        in_specs=[vmem, vmem, vmem, anywhere, anywhere],
        out_specs=(anywhere,) * 5,
        scratch_shapes=[full] * 4 + [pltpu.VMEM((rows, width), F32), pltpu.SemaphoreType.DMA((7,))],
        compiler_params=pltpu.CompilerParams(vmem_limit_bytes=60 * 1024 * 1024),
    )(mixed, query_grad, sums, key_act, value_act)


def solution(mesh):
    return jax.shard_map(
        per_device,
        mesh=mesh,
        in_specs=(P("seq", "ch"),) * 5 + (P("ch", None),),
        out_specs=(P("seq", "ch"),) * 5,
        check_vma=False,
    )
```

```python
import functools
import math

import jax
import jax.numpy as jnp
import numpy as np
from jax import lax
from jax.experimental import pallas as pl
from jax.experimental.pallas import tpu as pltpu
from jax.sharding import PartitionSpec as P

MESH = pl.DeviceIdType.MESH
F32 = jnp.float32
BF16 = jnp.bfloat16


NEAR = ((0, 1), (0, -1))
GATHER_ROUTES = ((1, 0), (0, 2)) + NEAR + NEAR + ((1, 0),)
GATHER_BLOCKS = ((0, 0),) * 4 + ((1, 0), (1, 0), (0, 2))
GATHER_PASSED = {0: (4, 5), 1: (6,)}
GATHER_SOURCES = ((1, 0), (0, 2), (0, -1), (0, 1), (1, -1), (1, 1), (1, 2))
EARLY = 2
GATHER_ORDER = (0, 1, 2, 3, 4, 5, 6)
SCATTER_ROUTES = ((1, 0),) + NEAR + NEAR + ((0, 2), (1, 0))
SCATTER_BLOCKS = ((1, 2), (1, 1), (1, -1), (0, 1), (0, -1), (0, 2), (1, 0))
SCATTER_ADDS = ((), (), (), (), (), (0,), (1, 2))
GREETED = ((1, 0), (0, 2)) + NEAR


def peers_far_first(seq, n_seq):
    if n_seq < 32:
        return [(seq + i) % n_seq for i in range(1, n_seq)]
    z_now, x_now, core_now = seq // 8, seq // 2 % 4, seq % 2
    z = [(z_now + d) % 4 * 8 for d in range(4)]
    x = [(x_now + d) % 4 * 2 for d in range(4)]
    core = [core_now, 1 - core_now]
    hops = sorted(
        (-(2 * min(dz, 4 - dz) + min(dx, 4 - dx)), -dc, dz, dx)
        for dz in range(4)
        for dx in range(4)
        for dc in range(2)
        if dz or dx or dc
    )
    return [z[dz] + x[dx] + core[-dc] for _, dc, dz, dx in hops]


def transform_tables(block_count, span_rows, own_channels):
    blocks = np.arange(block_count)
    times = np.arange(span_rows)
    across = 2.0 * math.pi * np.outer(2 * blocks + 1, blocks) / (4 * block_count)
    turn = 2.0 * math.pi * np.outer(2 * blocks + 1, times) / (4 * block_count * span_rows)
    within = 2.0 * math.pi * (np.outer(times, times) % span_rows) / span_rows
    each = np.eye(own_channels)
    across_fwd = np.concatenate([np.kron(np.cos(across), each), np.kron(-np.sin(across), each)], axis=0)
    across_inv = across_fwd.T / (block_count * span_rows)
    within_fwd = np.block([[np.cos(within), -np.sin(within)], [np.sin(within), np.cos(within)]])
    turn_cos = np.repeat(np.cos(turn), own_channels, axis=0)
    turn_sin = np.repeat(np.sin(turn), own_channels, axis=0)
    return (
        jnp.asarray(across_fwd, BF16),
        jnp.asarray(across_inv, BF16),
        jnp.asarray(within_fwd, BF16),
        jnp.asarray(within_fwd.T, BF16),
        jnp.asarray(turn_cos, F32),
        jnp.asarray(turn_sin, F32),
    )


def layer_kernel(
    n_seq,
    n_ch,
    q_hbm,
    k_hbm,
    v_hbm,
    h_hbm,
    og_hbm,
    w_hbm,
    kf_hbm,
    ki_hbm,
    df_hbm,
    di_hbm,
    tc_hbm,
    ts_hbm,
    mixed_ref,
    qg_ref,
    dd,
    q_ref,
    k_ref,
    v_ref,
    h_ref,
    og_ref,
    w,
    kf,
    ki,
    df,
    di,
    tc,
    ts,
    uh_src,
    uh,
    cv_src,
    cv,
    g_src,
    g,
    dd_src,
    og,
    rs_src,
    rs,
    level,
    spec_uh,
    spec_out,
    turned,
    gg,
    load_sem,
    send_sem,
    recv_sem,
    ag_send,
    ag_recv,
    rs_send,
    rs_recv,
):
    seq = lax.axis_index("seq")
    ch = lax.axis_index("ch")
    rows, width = q_hbm.shape
    lanes = rows
    half = n_seq * (width // n_seq)
    part = width
    step_rows = min(128, half)
    n_y = n_ch // 2
    plane, row = ch // n_y, ch % n_y

    def column(d_plane, d_row):
        return ((plane + d_plane) % 2) * n_y + (row + d_row) % n_y

    far_first = peers_far_first(seq, n_seq)

    loads = [
        pltpu.make_async_copy(src, dst, load_sem.at[i])
        for i, (src, dst) in enumerate(
            [
                (k_hbm, k_ref),
                (v_hbm, v_ref),
                (h_hbm, h_ref),
                (og_hbm, og_ref),
                (kf_hbm, kf),
                (tc_hbm, tc),
                (ts_hbm, ts),
                (df_hbm, df),
                (di_hbm, di),
                (ki_hbm, ki),
                (w_hbm, w),
                (q_hbm, q_ref),
            ]
        )
    ]
    for load in loads:
        load.start()

    barrier = pltpu.get_barrier_semaphore()

    with jax.named_scope("greet"):
        for peer in far_first:
            pl.semaphore_signal(barrier, inc=1, device_id={"seq": peer}, device_id_type=MESH)
        for d_plane, d_row in GREETED:
            pl.semaphore_signal(
                barrier, inc=1, device_id={"ch": column(d_plane, d_row)}, device_id_type=MESH
            )

    with jax.named_scope("product"):
        for load in loads[:3]:
            load.wait()
        u = (k_ref[...].astype(F32) * v_ref[...].astype(F32)).astype(BF16)
        uh_src[:, :, :lanes] = u.T.reshape(n_seq, width // n_seq, rows)
        uh_src[:, :, lanes:] = h_ref[...].T.reshape(n_seq, width // n_seq, rows)

    def grad_block(value, source):
        columns = pl.ds(pl.multiple_of(source * part, part), part)
        return lax.dot_general(value, w[:, columns], (((1,), (1,)), ((), ())), preferred_element_type=F32)

    with jax.named_scope("own_gate_grad"):
        loads[3].wait()
        loads[10].wait()
        gg[...] = grad_block(og_ref[...], ch)

    with jax.named_scope("barrier"):
        pl.semaphore_wait(barrier, n_seq - 1 + len(GREETED))

    def exchange(src, dst, slot):
        for peer in far_first:
            pltpu.make_async_remote_copy(
                src_ref=src.at[peer],
                dst_ref=dst.at[seq],
                send_sem=send_sem.at[slot],
                recv_sem=recv_sem.at[slot],
                device_id={"seq": peer},
                device_id_type=MESH,
            ).start()
        dst[seq] = src[seq]

    def arrived(dst, slot):
        landed = dst.at[pl.ds(0, n_seq - 1)]
        pltpu.make_async_copy(landed, landed, recv_sem.at[slot]).wait()

    def departed(src, slot):
        left = src.at[pl.ds(0, n_seq - 1)]
        pltpu.make_async_copy(left, left, send_sem.at[slot]).wait()

    def gather_copy(kind):
        moved = GATHER_BLOCKS[kind]
        block = column(*moved)
        return pltpu.make_async_remote_copy(
            src_ref=og_ref if moved == (0, 0) else og.at[block],
            dst_ref=og.at[block],
            send_sem=ag_send.at[kind],
            recv_sem=ag_recv.at[kind],
            device_id={"ch": column(*GATHER_ROUTES[kind])},
            device_id_type=MESH,
        )

    with jax.named_scope("send_uh_og"):
        for kind in range(4):
            gather_copy(kind).start()
        exchange(uh_src, uh, 0)
        for load in loads[4:10]:
            load.wait()
    def add_grad_block(kind):
        source = column(*GATHER_SOURCES[kind])
        gg[...] += grad_block(og[source], source)

    def collect(kinds):
        for kind in kinds:
            gather_copy(kind).wait_recv()
            for passed in GATHER_PASSED.get(kind, ()):
                gather_copy(passed).start()
            add_grad_block(kind)

    with jax.named_scope("gate_grad_early"):
        collect(GATHER_ORDER[:EARLY])

    def forward(values, count, put):
        level[:, : count * lanes] = jnp.dot(kf[...], values, preferred_element_type=F32)
        for r in range(0, half, step_rows):
            c, s = tc[r : r + step_rows, :], ts[r : r + step_rows, :]
            for a in range(count):
                re = level[r : r + step_rows, a * lanes : (a + 1) * lanes]
                im = level[half + r : half + r + step_rows, a * lanes : (a + 1) * lanes]
                z = jnp.concatenate([re * c + im * s, im * c - re * s], axis=1).astype(BF16)
                put(r, a, jnp.dot(z, df[...], preferred_element_type=F32))

    def inverse(product, count, dst):
        for r in range(0, half, step_rows):
            c, s = tc[r : r + step_rows, :], ts[r : r + step_rows, :]
            for a in range(count):
                x = jnp.dot(product(r, a), di[...], preferred_element_type=F32)
                re, im = x[:, :lanes], x[:, lanes:]
                turned[r : r + step_rows, a * lanes : (a + 1) * lanes] = (re * c - im * s).astype(BF16)
                turned[half + r : half + r + step_rows, a * lanes : (a + 1) * lanes] = (
                    im * c + re * s
                ).astype(BF16)
        y = jnp.dot(ki[...], turned[:, : count * lanes], preferred_element_type=F32)
        dst[...] = y.astype(BF16).reshape(dst.shape)

    def put_uh(r, a, value):
        spec_uh[a, r : r + step_rows, :] = value

    def conv_product(r, a):
        x, y = spec_uh[0, r : r + step_rows, :], spec_uh[1, r : r + step_rows, :]
        xr, xi, yr, yi = x[:, :lanes], x[:, lanes:], y[:, :lanes], y[:, lanes:]
        return jnp.concatenate([xr * yr - xi * yi, xr * yi + xi * yr], axis=1).astype(BF16)

    with jax.named_scope("wait_uh"):
        arrived(uh, 0)
    with jax.named_scope("forward_uh"):
        forward(uh[...].reshape(half, 2 * lanes), 2, put_uh)
    with jax.named_scope("inverse_conv"):
        inverse(conv_product, 1, cv_src)
    with jax.named_scope("send_conv"):
        exchange(cv_src, cv, 1)

    with jax.named_scope("gate_grad_late"):
        collect(GATHER_ORDER[EARLY:])
        loads[11].wait()

    with jax.named_scope("send_g"):
        conv_grad = (gg[...] * q_ref[...].astype(F32)).astype(BF16)
        g_src[...] = conv_grad.T.reshape(g_src.shape)
        exchange(g_src, g, 2)

    with jax.named_scope("wait_conv"):
        arrived(cv, 1)
    with jax.named_scope("gate"):
        conv = cv[...].reshape(width, rows).T.astype(F32)
        qg_ref[...] = (gg[...] * conv).astype(BF16)
        gated = (q_ref[...].astype(F32) * conv).astype(BF16)

    def scatter_copy(kind):
        return pltpu.make_async_remote_copy(
            src_ref=rs_src.at[kind],
            dst_ref=rs.at[kind],
            send_sem=rs_send.at[kind],
            recv_sem=rs_recv.at[kind],
            device_id={"ch": column(*SCATTER_ROUTES[kind])},
            device_id_type=MESH,
        )

    def out_block(target):
        columns = pl.ds(pl.multiple_of(target * part, part), part)
        return jnp.dot(gated, w[:, columns], preferred_element_type=F32)

    def send_block(kind):
        total = out_block(column(*SCATTER_BLOCKS[kind]))
        for earlier in SCATTER_ADDS[kind]:
            scatter_copy(earlier).wait_recv()
            total = total + rs[earlier].astype(F32)
        rs_src[kind] = total.astype(BF16)
        scatter_copy(kind).start()

    with jax.named_scope("out_blocks"):
        for kind in range(5):
            send_block(kind)

    def put_g(r, a, value):
        gr, gi = value[:, :lanes], value[:, lanes:]
        for b in range(2):
            x = spec_uh[1 - b, r : r + step_rows, :]
            xr, xi = x[:, :lanes], x[:, lanes:]
            spec_out[b, r : r + step_rows, :] = jnp.concatenate(
                [xr * gr + xi * gi, xr * gi - xi * gr], axis=1
            ).astype(BF16)

    with jax.named_scope("wait_g"):
        arrived(g, 2)
    with jax.named_scope("forward_g"):
        forward(g[...].reshape(half, lanes), 1, put_g)
    with jax.named_scope("inverse_grads"):
        inverse(lambda r, a: spec_out[a, r : r + step_rows, :], 2, dd_src)
    with jax.named_scope("send_grads"):
        exchange(dd_src, dd, 3)

    with jax.named_scope("mixed_sum"):
        send_block(5)
        send_block(6)
        total = out_block(ch)
        for kind in range(3, 7):
            scatter_copy(kind).wait_recv()
            total = total + rs[kind].astype(F32)
        mixed_ref[...] = total.astype(BF16)

    with jax.named_scope("wait_grads"):
        arrived(dd, 3)
    with jax.named_scope("departures"):
        departed(uh_src, 0)
        departed(cv_src, 1)
        departed(g_src, 2)
        departed(dd_src, 3)
        for kind in range(7):
            gather_copy(kind).wait_send()
            scatter_copy(kind).wait_send()


def finish_kernel(
    mixed_in, qg_in, dd, k_hbm, v_hbm, mixed_out, qg_out, kg_out, vg_out, fg_out, k_ref, v_ref, kg, vg, fg, sem
):
    n_seq, own, lanes = dd.shape
    rows, width = k_ref.shape
    lanes = lanes // 2
    first = [
        pltpu.make_async_copy(src, dst, sem.at[i])
        for i, (src, dst) in enumerate([(k_hbm, k_ref), (v_hbm, v_ref), (mixed_in, mixed_out), (qg_in, qg_out)])
    ]
    last = [
        pltpu.make_async_copy(src, dst, sem.at[4 + i])
        for i, (src, dst) in enumerate([(fg, fg_out), (kg, kg_out), (vg, vg_out)])
    ]
    for copy in first:
        copy.start()
    fg[...] = dd[:, :, lanes:].reshape(width, rows).T.astype(F32)
    last[0].start()
    u_grad = dd[:, :, :lanes].reshape(width, rows).T.astype(F32)
    first[0].wait()
    first[1].wait()
    kg[...] = (u_grad * v_ref[...].astype(F32)).astype(BF16)
    last[1].start()
    vg[...] = (u_grad * k_ref[...].astype(F32)).astype(BF16)
    last[2].start()
    for copy in first[2:] + last:
        copy.wait()


def per_device(query_act, key_act, value_act, filter_taps, out_grad, out_weight):
    rows, width = query_act.shape
    n_seq, n_ch = lax.axis_size("seq"), lax.axis_size("ch")
    own = width // n_seq
    tables = transform_tables(n_seq, rows, own)
    half = n_seq * own
    vmem, fixed = pl.BlockSpec(memory_space=pltpu.VMEM), pl.BlockSpec(memory_space=pltpu.HBM)
    bf = jax.ShapeDtypeStruct((rows, width), BF16)

    def blocks(lanes):
        return pltpu.VMEM((n_seq, own, lanes), BF16)

    full = pltpu.VMEM((rows, width), BF16)
    operands = (query_act, key_act, value_act, filter_taps, out_grad, out_weight, *tables)
    mixed, query_grad, sums = pl.pallas_call(
        functools.partial(layer_kernel, n_seq, n_ch),
        out_shape=(bf, bf, jax.ShapeDtypeStruct((n_seq, own, 2 * rows), BF16)),
        in_specs=[fixed] * 12,
        out_specs=(vmem,) * 3,
        scratch_shapes=[
            full,
            full,
            full,
            full,
            full,
            pltpu.VMEM(out_weight.shape, BF16),
            *[pltpu.VMEM(t.shape, t.dtype) for t in tables],
            blocks(2 * rows),
            blocks(2 * rows),
            blocks(rows),
            blocks(rows),
            blocks(rows),
            blocks(rows),
            blocks(2 * rows),
            pltpu.VMEM((n_ch, rows, width), BF16),
            pltpu.VMEM((7, rows, width), BF16),
            pltpu.VMEM((7, rows, width), BF16),
            pltpu.VMEM((2 * half, 2 * rows), F32),
            pltpu.VMEM((2, half, 2 * rows), F32),
            pltpu.VMEM((2, half, 2 * rows), BF16),
            pltpu.VMEM((2 * half, 2 * rows), BF16),
            pltpu.VMEM((rows, width), F32),
            pltpu.SemaphoreType.DMA((12,)),
            pltpu.SemaphoreType.DMA((4,)),
            pltpu.SemaphoreType.DMA((4,)),
            pltpu.SemaphoreType.DMA((7,)),
            pltpu.SemaphoreType.DMA((7,)),
            pltpu.SemaphoreType.DMA((7,)),
            pltpu.SemaphoreType.DMA((7,)),
        ],
        compiler_params=pltpu.CompilerParams(
            collective_id=0, has_side_effects=True, vmem_limit_bytes=32 * 1024 * 1024
        ),
    )(*[pltpu.with_memory_space_constraint(a, pltpu.HBM) for a in operands])
    return pl.pallas_call(
        finish_kernel,
        out_shape=(bf, bf, bf, bf, jax.ShapeDtypeStruct((rows, width), F32)),
        in_specs=[vmem, vmem, vmem, fixed, fixed],
        out_specs=(fixed,) * 5,
        scratch_shapes=[full] * 4 + [pltpu.VMEM((rows, width), F32), pltpu.SemaphoreType.DMA((7,))],
        compiler_params=pltpu.CompilerParams(vmem_limit_bytes=32 * 1024 * 1024),
    )(mixed, query_grad, sums, key_act, value_act)


def solution(mesh):
    return jax.shard_map(
        per_device,
        mesh=mesh,
        in_specs=(P("seq", "ch"),) * 5 + (P("ch", None),),
        out_specs=(P("seq", "ch"),) * 5,
        check_vma=False,
    )
```

```python
import functools
import math

import jax
import jax.numpy as jnp
import numpy as np
from jax import lax
from jax.experimental import pallas as pl
from jax.experimental.pallas import tpu as pltpu
from jax.sharding import PartitionSpec as P

MESH = pl.DeviceIdType.MESH
F32 = jnp.float32
BF16 = jnp.bfloat16


ALL, FIRST, SECOND = 0, 1, 2
UP, DOWN, ACROSS, FAR = (0, 1), (0, -1), (1, 0), (0, 2)
OWN = (0, 0)
GATHER_MOVES = (
    (OWN, ALL, ACROSS),
    (OWN, FIRST, FAR),
    (OWN, SECOND, FAR),
    (OWN, ALL, UP),
    (OWN, ALL, DOWN),
    (ACROSS, ALL, UP),
    (ACROSS, ALL, DOWN),
    (FAR, FIRST, ACROSS),
    (FAR, SECOND, ACROSS),
)
GATHER_PASSED = {0: (5, 6), 1: (7,), 2: (8,)}
GATHER_SOURCES = {0: ACROSS, 2: FAR, 3: DOWN, 4: UP, 5: (1, -1), 6: (1, 1), 8: (1, 2)}
EARLY = 5
SCATTER_MOVES = (
    ((1, 2), ALL, ACROSS),
    ((1, 1), ALL, UP),
    ((1, -1), ALL, DOWN),
    (UP, ALL, UP),
    (DOWN, ALL, DOWN),
    (FAR, ALL, FAR),
    (ACROSS, ALL, ACROSS),
)
SCATTER_ADDS = {5: (0,), 6: (1, 2)}
BEFORE = 5
SCATTER_LAST = (3, 4, 5, 6)
GREETED = (ACROSS, FAR, UP, DOWN)


def peers_far_first(seq, n_seq):
    if n_seq < 32:
        return [(seq + i) % n_seq for i in range(1, n_seq)]
    z_now, x_now, core_now = seq // 8, seq // 2 % 4, seq % 2
    z = [(z_now + d) % 4 * 8 for d in range(4)]
    x = [(x_now + d) % 4 * 2 for d in range(4)]
    core = [core_now, 1 - core_now]
    hops = sorted(
        (-(2 * min(dz, 4 - dz) + min(dx, 4 - dx)), -dc, dz, dx)
        for dz in range(4)
        for dx in range(4)
        for dc in range(2)
        if dz or dx or dc
    )
    return [z[dz] + x[dx] + core[-dc] for _, dc, dz, dx in hops]


def transform_tables(block_count, span_rows, own_channels):
    blocks = np.arange(block_count)
    times = np.arange(span_rows)
    across = 2.0 * math.pi * np.outer(2 * blocks + 1, blocks) / (4 * block_count)
    turn = 2.0 * math.pi * np.outer(2 * blocks + 1, times) / (4 * block_count * span_rows)
    within = 2.0 * math.pi * (np.outer(times, times) % span_rows) / span_rows
    each = np.eye(own_channels)
    across_fwd = np.concatenate([np.kron(np.cos(across), each), np.kron(-np.sin(across), each)], axis=0)
    across_inv = across_fwd.T / (block_count * span_rows)
    within_fwd = np.block([[np.cos(within), -np.sin(within)], [np.sin(within), np.cos(within)]])
    turn_cos = np.repeat(np.cos(turn), own_channels, axis=0)
    turn_sin = np.repeat(np.sin(turn), own_channels, axis=0)
    return (
        jnp.asarray(across_fwd, BF16),
        jnp.asarray(across_inv, BF16),
        jnp.asarray(within_fwd, BF16),
        jnp.asarray(within_fwd.T, BF16),
        jnp.asarray(turn_cos, F32),
        jnp.asarray(turn_sin, F32),
    )


def layer_kernel(
    n_seq,
    n_ch,
    q_hbm,
    k_hbm,
    v_hbm,
    h_hbm,
    og_hbm,
    w_hbm,
    kf_hbm,
    ki_hbm,
    df_hbm,
    di_hbm,
    tc_hbm,
    ts_hbm,
    mixed_ref,
    qg_ref,
    du,
    dh,
    q_ref,
    k_ref,
    v_ref,
    h_ref,
    og_ref,
    w,
    kf,
    ki,
    df,
    di,
    tc,
    ts,
    uh_src,
    uh,
    cv_src,
    cv,
    g_src,
    g,
    du_src,
    dh_src,
    og,
    rs_src,
    rs,
    level,
    spec_uh,
    spec_out,
    turned,
    gg,
    q_turned,
    load_sem,
    send_sem,
    recv_sem,
    ag_send,
    ag_recv,
    rs_send,
    rs_recv,
):
    seq = lax.axis_index("seq")
    ch = lax.axis_index("ch")
    rows, width = q_hbm.shape
    lanes = rows
    half = n_seq * (width // n_seq)
    part = width
    step_rows = min(128, half)
    n_y = n_ch // 2
    plane, row = ch // n_y, ch % n_y

    def column(d_plane, d_row):
        return ((plane + d_plane) % 2) * n_y + (row + d_row) % n_y

    far_first = peers_far_first(seq, n_seq)
    some_rows = (pl.ds(0, rows), pl.ds(0, rows // 2), pl.ds(rows // 2, rows // 2))

    barrier = pltpu.get_barrier_semaphore()

    with jax.named_scope("greet"):
        for peer in far_first:
            pl.semaphore_signal(barrier, inc=1, device_id={"seq": peer}, device_id_type=MESH)
        for d_plane, d_row in GREETED:
            pl.semaphore_signal(
                barrier, inc=1, device_id={"ch": column(d_plane, d_row)}, device_id_type=MESH
            )

    loads = [
        pltpu.make_async_copy(src, dst, load_sem.at[i])
        for i, (src, dst) in enumerate(
            [
                (k_hbm, k_ref),
                (v_hbm, v_ref),
                (h_hbm, h_ref),
                (og_hbm, og_ref),
                (kf_hbm, kf),
                (tc_hbm, tc),
                (ts_hbm, ts),
                (df_hbm, df),
                (di_hbm, di),
                (ki_hbm, ki),
                (w_hbm, w),
                (q_hbm, q_ref),
            ]
        )
    ]
    for load in loads:
        load.start()

    with jax.named_scope("product"):
        for load in loads[:3]:
            load.wait()
        u = (k_ref[...].astype(F32) * v_ref[...].astype(F32)).astype(BF16)
        uh_src[:, :, :lanes] = u.T.reshape(n_seq, width // n_seq, rows)
        uh_src[:, :, lanes:] = h_ref[...].T.reshape(n_seq, width // n_seq, rows)

    def grad_block(value, source):
        columns = pl.ds(pl.multiple_of(source * part, part), part)
        return lax.dot_general(w[:, columns], value, (((1,), (1,)), ((), ())), preferred_element_type=F32)

    with jax.named_scope("own_gate_grad"):
        loads[11].wait()
        q_turned[...] = q_ref[...].T
        loads[3].wait()
        loads[10].wait()
        gg[...] = grad_block(og_ref[...], ch)

    with jax.named_scope("barrier"):
        pl.semaphore_wait(barrier, n_seq - 1 + len(GREETED))

    def exchange(src, dst, slot):
        for peer in far_first:
            pltpu.make_async_remote_copy(
                src_ref=src.at[peer],
                dst_ref=dst.at[seq],
                send_sem=send_sem.at[slot],
                recv_sem=recv_sem.at[slot],
                device_id={"seq": peer},
                device_id_type=MESH,
            ).start()
        dst[seq] = src[seq]

    def arrived(dst, slot):
        landed = dst.at[pl.ds(0, n_seq - 1)]
        pltpu.make_async_copy(landed, landed, recv_sem.at[slot]).wait()

    def departed(src, slot):
        left = src.at[pl.ds(0, n_seq - 1)]
        pltpu.make_async_copy(left, left, send_sem.at[slot]).wait()

    def gather_copy(kind):
        moved, extent, goal = GATHER_MOVES[kind]
        block, extent = column(*moved), some_rows[extent]
        return pltpu.make_async_remote_copy(
            src_ref=og_ref.at[extent] if moved == OWN else og.at[block, extent],
            dst_ref=og.at[block, extent],
            send_sem=ag_send.at[kind],
            recv_sem=ag_recv.at[kind],
            device_id={"ch": column(*goal)},
            device_id_type=MESH,
        )

    with jax.named_scope("send_uh_og"):
        for kind in [i for i, move in enumerate(GATHER_MOVES) if move[0] == OWN]:
            gather_copy(kind).start()
        exchange(uh_src, uh, 0)
        for load in loads[4:10]:
            load.wait()
    def add_grad_block(kind):
        source = column(*GATHER_SOURCES[kind])
        gg[...] += grad_block(og[source], source)

    def collect(kinds):
        for kind in kinds:
            gather_copy(kind).wait_recv()
            for passed in GATHER_PASSED.get(kind, ()):
                gather_copy(passed).start()
            if kind in GATHER_SOURCES:
                add_grad_block(kind)

    with jax.named_scope("gate_grad_early"):
        collect(range(EARLY))

    def forward(values, count, put):
        level[:, : count * lanes] = jnp.dot(kf[...], values, preferred_element_type=F32)
        for r in range(0, half, step_rows):
            c, s = tc[r : r + step_rows, :], ts[r : r + step_rows, :]
            for a in range(count):
                re = level[r : r + step_rows, a * lanes : (a + 1) * lanes]
                im = level[half + r : half + r + step_rows, a * lanes : (a + 1) * lanes]
                z = jnp.concatenate([re * c + im * s, im * c - re * s], axis=1).astype(BF16)
                put(r, a, jnp.dot(z, df[...], preferred_element_type=F32))

    def inverse(product, count, dst):
        for r in range(0, half, step_rows):
            c, s = tc[r : r + step_rows, :], ts[r : r + step_rows, :]
            for a in range(count):
                x = jnp.dot(product(r, a), di[...], preferred_element_type=F32)
                re, im = x[:, :lanes], x[:, lanes:]
                turned[r : r + step_rows, a * lanes : (a + 1) * lanes] = (re * c - im * s).astype(BF16)
                turned[half + r : half + r + step_rows, a * lanes : (a + 1) * lanes] = (
                    im * c + re * s
                ).astype(BF16)
        y = jnp.dot(ki[...], turned[:, : count * lanes], preferred_element_type=F32)
        dst[...] = y.astype(BF16).reshape(dst.shape)

    def put_uh(r, a, value):
        spec_uh[a, r : r + step_rows, :] = value

    def conv_product(r, a):
        x, y = spec_uh[0, r : r + step_rows, :], spec_uh[1, r : r + step_rows, :]
        xr, xi, yr, yi = x[:, :lanes], x[:, lanes:], y[:, :lanes], y[:, lanes:]
        return jnp.concatenate([xr * yr - xi * yi, xr * yi + xi * yr], axis=1).astype(BF16)

    with jax.named_scope("wait_uh"):
        arrived(uh, 0)
    with jax.named_scope("forward_uh"):
        forward(uh[...].reshape(half, 2 * lanes), 2, put_uh)
    with jax.named_scope("inverse_conv"):
        inverse(conv_product, 1, cv_src)
    with jax.named_scope("send_conv"):
        exchange(cv_src, cv, 1)

    with jax.named_scope("gate_grad_late"):
        collect(range(EARLY, len(GATHER_MOVES)))

    with jax.named_scope("send_g"):
        conv_grad = (gg[...] * q_turned[...].astype(F32)).astype(BF16)
        g_src[...] = conv_grad.reshape(g_src.shape)
        exchange(g_src, g, 2)

    with jax.named_scope("wait_conv"):
        arrived(cv, 1)
    with jax.named_scope("gate"):
        conv = cv[...].reshape(width, rows).T.astype(F32)
        gated = (q_ref[...].astype(F32) * conv).astype(BF16)

    def scatter_copy(kind):
        _, extent, goal = SCATTER_MOVES[kind]
        extent = some_rows[extent]
        return pltpu.make_async_remote_copy(
            src_ref=rs_src.at[kind, extent],
            dst_ref=rs.at[kind, extent],
            send_sem=rs_send.at[kind],
            recv_sem=rs_recv.at[kind],
            device_id={"ch": column(*goal)},
            device_id_type=MESH,
        )

    def out_block(target):
        columns = pl.ds(pl.multiple_of(target * part, part), part)
        return jnp.dot(gated, w[:, columns], preferred_element_type=F32)

    def send_block(kind):
        total = out_block(column(*SCATTER_MOVES[kind][0]))
        for earlier in SCATTER_ADDS.get(kind, ()):
            scatter_copy(earlier).wait_recv()
            total = total + rs[earlier].astype(F32)
        rs_src[kind] = total.astype(BF16)
        scatter_copy(kind).start()

    with jax.named_scope("out_blocks"):
        for kind in range(BEFORE):
            send_block(kind)

    def put_g(r, a, value):
        gr, gi = value[:, :lanes], value[:, lanes:]
        for b in range(2):
            x = spec_uh[1 - b, r : r + step_rows, :]
            xr, xi = x[:, :lanes], x[:, lanes:]
            spec_out[b, r : r + step_rows, :] = jnp.concatenate(
                [xr * gr + xi * gi, xr * gi - xi * gr], axis=1
            ).astype(BF16)

    with jax.named_scope("wait_g"):
        arrived(g, 2)
    with jax.named_scope("forward_g"):
        forward(g[...].reshape(half, lanes), 1, put_g)
    for b, (src, dst) in enumerate(((du_src, du), (dh_src, dh))):
        with jax.named_scope("inverse_grads"):
            inverse(lambda r, a: spec_out[b, r : r + step_rows, :], 1, src)
        with jax.named_scope("send_grads"):
            exchange(src, dst, 3 + b)

    with jax.named_scope("mixed_sum"):
        for kind in (6, 5):
            send_block(kind)
        with jax.named_scope("query_grad"):
            query_grad = (gg[...] * cv[...].reshape(width, rows).astype(F32)).astype(BF16)
            qg_ref[...] = query_grad.T
        total = out_block(ch)
        for kind in SCATTER_LAST:
            scatter_copy(kind).wait_recv()
            total = total + rs[kind].astype(F32)
        mixed_ref[...] = total.astype(BF16)

    with jax.named_scope("wait_grads"):
        arrived(du, 3)
        arrived(dh, 4)
    with jax.named_scope("departures"):
        departed(uh_src, 0)
        departed(cv_src, 1)
        departed(g_src, 2)
        departed(du_src, 3)
        departed(dh_src, 4)
        for kind in range(len(GATHER_MOVES)):
            gather_copy(kind).wait_send()
        for kind in range(len(SCATTER_MOVES)):
            scatter_copy(kind).wait_send()


def finish_kernel(
    mixed_in, qg_in, du, dh, k_hbm, v_hbm, mixed_out, qg_out, kg_out, vg_out, fg_out, k_ref, v_ref, kg, vg, fg, sem
):
    rows, width = k_ref.shape
    first = [
        pltpu.make_async_copy(src, dst, sem.at[i])
        for i, (src, dst) in enumerate([(k_hbm, k_ref), (v_hbm, v_ref), (mixed_in, mixed_out), (qg_in, qg_out)])
    ]
    last = [
        pltpu.make_async_copy(src, dst, sem.at[4 + i])
        for i, (src, dst) in enumerate([(fg, fg_out), (kg, kg_out), (vg, vg_out)])
    ]
    for copy in first:
        copy.start()
    fg[...] = dh[...].reshape(width, rows).T.astype(F32)
    last[0].start()
    u_grad = du[...].reshape(width, rows).T.astype(F32)
    first[0].wait()
    first[1].wait()
    kg[...] = (u_grad * v_ref[...].astype(F32)).astype(BF16)
    last[1].start()
    vg[...] = (u_grad * k_ref[...].astype(F32)).astype(BF16)
    last[2].start()
    for copy in first[2:] + last:
        copy.wait()


def per_device(query_act, key_act, value_act, filter_taps, out_grad, out_weight):
    rows, width = query_act.shape
    n_seq, n_ch = lax.axis_size("seq"), lax.axis_size("ch")
    own = width // n_seq
    tables = transform_tables(n_seq, rows, own)
    half = n_seq * own
    vmem, fixed = pl.BlockSpec(memory_space=pltpu.VMEM), pl.BlockSpec(memory_space=pltpu.HBM)
    bf = jax.ShapeDtypeStruct((rows, width), BF16)

    def blocks(lanes):
        return pltpu.VMEM((n_seq, own, lanes), BF16)

    full = pltpu.VMEM((rows, width), BF16)
    operands = (query_act, key_act, value_act, filter_taps, out_grad, out_weight, *tables)
    mixed, query_grad, u_grad, filter_grad = pl.pallas_call(
        functools.partial(layer_kernel, n_seq, n_ch),
        out_shape=(bf, bf, *[jax.ShapeDtypeStruct((n_seq, own, rows), BF16)] * 2),
        in_specs=[fixed] * 12,
        out_specs=(vmem,) * 4,
        scratch_shapes=[
            full,
            full,
            full,
            full,
            full,
            pltpu.VMEM(out_weight.shape, BF16),
            *[pltpu.VMEM(t.shape, t.dtype) for t in tables],
            blocks(2 * rows),
            blocks(2 * rows),
            blocks(rows),
            blocks(rows),
            blocks(rows),
            blocks(rows),
            blocks(rows),
            blocks(rows),
            pltpu.VMEM((n_ch, rows, width), BF16),
            pltpu.VMEM((len(SCATTER_MOVES), rows, width), BF16),
            pltpu.VMEM((len(SCATTER_MOVES), rows, width), BF16),
            pltpu.VMEM((2 * half, 2 * rows), F32),
            pltpu.VMEM((2, half, 2 * rows), F32),
            pltpu.VMEM((2, half, 2 * rows), BF16),
            pltpu.VMEM((2 * half, 2 * rows), BF16),
            pltpu.VMEM((width, rows), F32),
            pltpu.VMEM((width, rows), BF16),
            pltpu.SemaphoreType.DMA((12,)),
            pltpu.SemaphoreType.DMA((5,)),
            pltpu.SemaphoreType.DMA((5,)),
            pltpu.SemaphoreType.DMA((len(GATHER_MOVES),)),
            pltpu.SemaphoreType.DMA((len(GATHER_MOVES),)),
            pltpu.SemaphoreType.DMA((len(SCATTER_MOVES),)),
            pltpu.SemaphoreType.DMA((len(SCATTER_MOVES),)),
        ],
        compiler_params=pltpu.CompilerParams(
            collective_id=0, has_side_effects=True, vmem_limit_bytes=32 * 1024 * 1024
        ),
    )(*[pltpu.with_memory_space_constraint(a, pltpu.HBM) for a in operands])
    return pl.pallas_call(
        finish_kernel,
        out_shape=(bf, bf, bf, bf, jax.ShapeDtypeStruct((rows, width), F32)),
        in_specs=[vmem, vmem, vmem, vmem, fixed, fixed],
        out_specs=(fixed,) * 5,
        scratch_shapes=[full] * 4 + [pltpu.VMEM((rows, width), F32), pltpu.SemaphoreType.DMA((7,))],
        compiler_params=pltpu.CompilerParams(vmem_limit_bytes=32 * 1024 * 1024),
    )(mixed, query_grad, u_grad, filter_grad, key_act, value_act)


def solution(mesh):
    return jax.shard_map(
        per_device,
        mesh=mesh,
        in_specs=(P("seq", "ch"),) * 5 + (P("ch", None),),
        out_specs=(P("seq", "ch"),) * 5,
        check_vma=False,
    )
```

```python
import functools
import math

import jax
import jax.numpy as jnp
import numpy as np
from jax import lax
from jax.experimental import pallas as pl
from jax.experimental.pallas import tpu as pltpu
from jax.sharding import PartitionSpec as P

MESH = pl.DeviceIdType.MESH
F32 = jnp.float32
BF16 = jnp.bfloat16


ALL, FIRST, SECOND = 0, 1, 2
UP, DOWN, ACROSS, FAR = (0, 1), (0, -1), (1, 0), (0, 2)
OWN = (0, 0)
GATHER_MOVES = (
    (OWN, ALL, ACROSS),
    (OWN, FIRST, FAR),
    (OWN, SECOND, FAR),
    (OWN, ALL, UP),
    (OWN, ALL, DOWN),
    (ACROSS, ALL, UP),
    (ACROSS, ALL, DOWN),
    (FAR, FIRST, ACROSS),
    (FAR, SECOND, ACROSS),
)
GATHER_PASSED = {0: (5, 6), 1: (7,), 2: (8,)}
GATHER_SOURCES = {0: ACROSS, 2: FAR, 3: DOWN, 4: UP, 5: (1, -1), 6: (1, 1), 8: (1, 2)}
EARLY = 5
SCATTER_MOVES = (
    ((1, 2), ALL, ACROSS),
    ((1, 1), ALL, UP),
    ((1, -1), ALL, DOWN),
    (UP, ALL, UP),
    (DOWN, ALL, DOWN),
    (FAR, ALL, FAR),
    (ACROSS, ALL, ACROSS),
)
SCATTER_ADDS = {5: (0,), 6: (1, 2)}
BEFORE = 5
SCATTER_LAST = (3, 4, 5, 6)
GREETED = (ACROSS, FAR, UP, DOWN)


def peers_far_first(seq, n_seq):
    if n_seq < 32:
        return [(seq + i) % n_seq for i in range(1, n_seq)]
    z_now, x_now, core_now = seq // 8, seq // 2 % 4, seq % 2
    z = [(z_now + d) % 4 * 8 for d in range(4)]
    x = [(x_now + d) % 4 * 2 for d in range(4)]
    core = [core_now, 1 - core_now]
    hops = sorted(
        (-(2 * min(dz, 4 - dz) + min(dx, 4 - dx)), -dc, dz, dx)
        for dz in range(4)
        for dx in range(4)
        for dc in range(2)
        if dz or dx or dc
    )
    return [z[dz] + x[dx] + core[-dc] for _, dc, dz, dx in hops]


def transform_tables(block_count, span_rows, own_channels):
    blocks = np.arange(block_count)
    times = np.arange(span_rows)
    across = 2.0 * math.pi * np.outer(2 * blocks + 1, blocks) / (4 * block_count)
    turn = 2.0 * math.pi * np.outer(2 * blocks + 1, times) / (4 * block_count * span_rows)
    within = 2.0 * math.pi * (np.outer(times, times) % span_rows) / span_rows
    each = np.eye(own_channels)
    across_fwd = np.concatenate([np.kron(np.cos(across), each), np.kron(-np.sin(across), each)], axis=0)
    across_inv = across_fwd.T / (block_count * span_rows)
    within_fwd = np.block([[np.cos(within), -np.sin(within)], [np.sin(within), np.cos(within)]])
    turn_cos = np.repeat(np.cos(turn), own_channels, axis=0)
    turn_sin = np.repeat(np.sin(turn), own_channels, axis=0)
    return (
        jnp.asarray(across_fwd, BF16),
        jnp.asarray(across_inv, BF16),
        jnp.asarray(within_fwd, BF16),
        jnp.asarray(within_fwd.T, BF16),
        jnp.asarray(turn_cos, F32),
        jnp.asarray(turn_sin, F32),
    )


def layer_kernel(
    n_seq,
    n_ch,
    q_hbm,
    k_hbm,
    v_hbm,
    h_hbm,
    og_hbm,
    w_hbm,
    kf_hbm,
    ki_hbm,
    df_hbm,
    di_hbm,
    tc_hbm,
    ts_hbm,
    mixed_ref,
    qg_ref,
    du,
    dh,
    q_ref,
    k_ref,
    v_ref,
    h_ref,
    og_ref,
    w,
    kf,
    ki,
    df,
    di,
    tc,
    ts,
    uh_src,
    uh,
    cv_src,
    cv,
    g_src,
    g,
    du_src,
    dh_src,
    og,
    rs_src,
    rs,
    level,
    spec_uh,
    spec_out,
    turned,
    gg,
    q_turned,
    load_sem,
    send_sem,
    recv_sem,
    ag_send,
    ag_recv,
    rs_send,
    rs_recv,
):
    seq = lax.axis_index("seq")
    ch = lax.axis_index("ch")
    rows, width = q_hbm.shape
    lanes = rows
    half = n_seq * (width // n_seq)
    part = width
    step_rows = min(128, half)
    n_y = n_ch // 2
    plane, row = ch // n_y, ch % n_y

    def column(d_plane, d_row):
        return ((plane + d_plane) % 2) * n_y + (row + d_row) % n_y

    far_first = peers_far_first(seq, n_seq)
    some_rows = (pl.ds(0, rows), pl.ds(0, rows // 2), pl.ds(rows // 2, rows // 2))

    barrier = pltpu.get_barrier_semaphore()

    with jax.named_scope("greet"):
        for peer in far_first:
            pl.semaphore_signal(barrier, inc=1, device_id={"seq": peer}, device_id_type=MESH)
        for d_plane, d_row in GREETED:
            pl.semaphore_signal(
                barrier, inc=1, device_id={"ch": column(d_plane, d_row)}, device_id_type=MESH
            )

    loads = [
        pltpu.make_async_copy(src, dst, load_sem.at[i])
        for i, (src, dst) in enumerate(
            [
                (k_hbm, k_ref),
                (v_hbm, v_ref),
                (h_hbm, h_ref),
                (og_hbm, og_ref),
                (kf_hbm, kf),
                (tc_hbm, tc),
                (ts_hbm, ts),
                (df_hbm, df),
                (di_hbm, di),
                (ki_hbm, ki),
                (w_hbm, w),
                (q_hbm, q_ref),
            ]
        )
    ]
    for load in loads:
        load.start()

    with jax.named_scope("product"):
        for load in loads[:3]:
            load.wait()
        u = (k_ref[...].astype(F32) * v_ref[...].astype(F32)).astype(BF16)
        uh_src[:, :, :lanes] = u.T.reshape(n_seq, width // n_seq, rows)
        uh_src[:, :, lanes:] = h_ref[...].T.reshape(n_seq, width // n_seq, rows)

    def grad_block(value, source):
        columns = pl.ds(pl.multiple_of(source * part, part), part)
        return lax.dot_general(w[:, columns], value, (((1,), (1,)), ((), ())), preferred_element_type=F32)

    with jax.named_scope("own_gate_grad"):
        loads[11].wait()
        q_turned[...] = q_ref[...].T
        loads[3].wait()
        loads[10].wait()
        gg[...] = grad_block(og_ref[...], ch)

    with jax.named_scope("barrier"):
        pl.semaphore_wait(barrier, n_seq - 1 + len(GREETED))

    def exchange(src, dst, slot):
        for peer in far_first:
            pltpu.make_async_remote_copy(
                src_ref=src.at[peer],
                dst_ref=dst.at[seq],
                send_sem=send_sem.at[slot],
                recv_sem=recv_sem.at[slot],
                device_id={"seq": peer},
                device_id_type=MESH,
            ).start()
        dst[seq] = src[seq]

    def arrived(dst, slot):
        landed = dst.at[pl.ds(0, n_seq - 1)]
        pltpu.make_async_copy(landed, landed, recv_sem.at[slot]).wait()

    def departed(src, slot):
        left = src.at[pl.ds(0, n_seq - 1)]
        pltpu.make_async_copy(left, left, send_sem.at[slot]).wait()

    def gather_copy(kind):
        moved, extent, goal = GATHER_MOVES[kind]
        block, extent = column(*moved), some_rows[extent]
        return pltpu.make_async_remote_copy(
            src_ref=og_ref.at[extent] if moved == OWN else og.at[block, extent],
            dst_ref=og.at[block, extent],
            send_sem=ag_send.at[kind],
            recv_sem=ag_recv.at[kind],
            device_id={"ch": column(*goal)},
            device_id_type=MESH,
        )

    with jax.named_scope("send_uh_og"):
        for kind in [i for i, move in enumerate(GATHER_MOVES) if move[0] == OWN]:
            gather_copy(kind).start()
        exchange(uh_src, uh, 0)
        for load in loads[4:10]:
            load.wait()
    def add_grad_block(kind):
        source = column(*GATHER_SOURCES[kind])
        gg[...] += grad_block(og[source], source)

    def collect(kinds):
        for kind in kinds:
            gather_copy(kind).wait_recv()
            for passed in GATHER_PASSED.get(kind, ()):
                gather_copy(passed).start()
            if kind in GATHER_SOURCES:
                add_grad_block(kind)

    with jax.named_scope("gate_grad_early"):
        collect(range(EARLY))

    def forward(values, count, put):
        level[:, : count * lanes] = jnp.dot(kf[...], values, preferred_element_type=F32)
        for r in range(0, half, step_rows):
            c, s = tc[r : r + step_rows, :], ts[r : r + step_rows, :]
            for a in range(count):
                re = level[r : r + step_rows, a * lanes : (a + 1) * lanes]
                im = level[half + r : half + r + step_rows, a * lanes : (a + 1) * lanes]
                z = jnp.concatenate([re * c + im * s, im * c - re * s], axis=1).astype(BF16)
                put(r, a, jnp.dot(z, df[...], preferred_element_type=F32))

    def inverse(product, count, dst):
        for r in range(0, half, step_rows):
            c, s = tc[r : r + step_rows, :], ts[r : r + step_rows, :]
            for a in range(count):
                x = jnp.dot(product(r, a), di[...], preferred_element_type=F32)
                re, im = x[:, :lanes], x[:, lanes:]
                turned[r : r + step_rows, a * lanes : (a + 1) * lanes] = (re * c - im * s).astype(BF16)
                turned[half + r : half + r + step_rows, a * lanes : (a + 1) * lanes] = (
                    im * c + re * s
                ).astype(BF16)
        y = jnp.dot(ki[...], turned[:, : count * lanes], preferred_element_type=F32)
        dst[...] = y.astype(BF16).reshape(dst.shape)

    def put_uh(r, a, value):
        spec_uh[a, r : r + step_rows, :] = value

    def conv_product(r, a):
        x, y = spec_uh[0, r : r + step_rows, :], spec_uh[1, r : r + step_rows, :]
        xr, xi, yr, yi = x[:, :lanes], x[:, lanes:], y[:, :lanes], y[:, lanes:]
        return jnp.concatenate([xr * yr - xi * yi, xr * yi + xi * yr], axis=1).astype(BF16)

    with jax.named_scope("wait_uh"):
        arrived(uh, 0)
    with jax.named_scope("forward_uh"):
        forward(uh[...].reshape(half, 2 * lanes), 2, put_uh)
    with jax.named_scope("inverse_conv"):
        inverse(conv_product, 1, cv_src)
    with jax.named_scope("send_conv"):
        exchange(cv_src, cv, 1)

    with jax.named_scope("gate_grad_late"):
        collect(range(EARLY, len(GATHER_MOVES)))

    with jax.named_scope("send_g"):
        conv_grad = (gg[...] * q_turned[...].astype(F32)).astype(BF16)
        g_src[...] = conv_grad.reshape(g_src.shape)
        exchange(g_src, g, 2)

    with jax.named_scope("wait_conv"):
        arrived(cv, 1)
    with jax.named_scope("gate"):
        conv = cv[...].reshape(width, rows).T.astype(F32)
        gated = (q_ref[...].astype(F32) * conv).astype(BF16)

    def scatter_copy(kind):
        _, extent, goal = SCATTER_MOVES[kind]
        extent = some_rows[extent]
        return pltpu.make_async_remote_copy(
            src_ref=rs_src.at[kind, extent],
            dst_ref=rs.at[kind, extent],
            send_sem=rs_send.at[kind],
            recv_sem=rs_recv.at[kind],
            device_id={"ch": column(*goal)},
            device_id_type=MESH,
        )

    def out_block(target):
        columns = pl.ds(pl.multiple_of(target * part, part), part)
        return jnp.dot(gated, w[:, columns], preferred_element_type=F32)

    def send_block(kind):
        total = out_block(column(*SCATTER_MOVES[kind][0]))
        for earlier in SCATTER_ADDS.get(kind, ()):
            scatter_copy(earlier).wait_recv()
            total = total + rs[earlier].astype(F32)
        rs_src[kind] = total.astype(BF16)
        scatter_copy(kind).start()

    with jax.named_scope("out_blocks"):
        for kind in (1, 2, 0, 3, 4):
            send_block(kind)

    def put_g(r, a, value):
        gr, gi = value[:, :lanes], value[:, lanes:]
        for b in range(2):
            x = spec_uh[1 - b, r : r + step_rows, :]
            xr, xi = x[:, :lanes], x[:, lanes:]
            spec_out[b, r : r + step_rows, :] = jnp.concatenate(
                [xr * gr + xi * gi, xr * gi - xi * gr], axis=1
            ).astype(BF16)

    with jax.named_scope("wait_g"):
        arrived(g, 2)
    with jax.named_scope("forward_g"):
        forward(g[...].reshape(half, lanes), 1, put_g)
    for b, (src, dst) in enumerate(((du_src, du), (dh_src, dh))):
        with jax.named_scope("inverse_grads"):
            inverse(lambda r, a: spec_out[b, r : r + step_rows, :], 1, src)
        with jax.named_scope("send_grads"):
            exchange(src, dst, 3 + b)

    with jax.named_scope("mixed_sum"):
        for kind in (6, 5):
            send_block(kind)
        with jax.named_scope("query_grad"):
            query_grad = (gg[...] * cv[...].reshape(width, rows).astype(F32)).astype(BF16)
            qg_ref[...] = query_grad.T
        total = out_block(ch)
        for kind in SCATTER_LAST:
            scatter_copy(kind).wait_recv()
            total = total + rs[kind].astype(F32)
        mixed_ref[...] = total.astype(BF16)

    with jax.named_scope("wait_grads"):
        arrived(du, 3)
        arrived(dh, 4)
    with jax.named_scope("departures"):
        departed(uh_src, 0)
        departed(cv_src, 1)
        departed(g_src, 2)
        departed(du_src, 3)
        departed(dh_src, 4)
        for kind in range(len(GATHER_MOVES)):
            gather_copy(kind).wait_send()
        for kind in range(len(SCATTER_MOVES)):
            scatter_copy(kind).wait_send()


def finish_kernel(
    mixed_in, qg_in, du, dh, k_hbm, v_hbm, mixed_out, qg_out, kg_out, vg_out, fg_out, k_ref, v_ref, kg, vg, fg, sem
):
    rows, width = k_ref.shape
    first = [
        pltpu.make_async_copy(src, dst, sem.at[i])
        for i, (src, dst) in enumerate([(k_hbm, k_ref), (v_hbm, v_ref), (mixed_in, mixed_out), (qg_in, qg_out)])
    ]
    last = [
        pltpu.make_async_copy(src, dst, sem.at[4 + i])
        for i, (src, dst) in enumerate([(fg, fg_out), (kg, kg_out), (vg, vg_out)])
    ]
    for copy in first:
        copy.start()
    fg[...] = dh[...].reshape(width, rows).T.astype(F32)
    last[0].start()
    u_grad = du[...].reshape(width, rows).T.astype(F32)
    first[0].wait()
    first[1].wait()
    kg[...] = (u_grad * v_ref[...].astype(F32)).astype(BF16)
    last[1].start()
    vg[...] = (u_grad * k_ref[...].astype(F32)).astype(BF16)
    last[2].start()
    for copy in first[2:] + last:
        copy.wait()


def per_device(query_act, key_act, value_act, filter_taps, out_grad, out_weight):
    rows, width = query_act.shape
    n_seq, n_ch = lax.axis_size("seq"), lax.axis_size("ch")
    own = width // n_seq
    tables = transform_tables(n_seq, rows, own)
    half = n_seq * own
    vmem, fixed = pl.BlockSpec(memory_space=pltpu.VMEM), pl.BlockSpec(memory_space=pltpu.HBM)
    bf = jax.ShapeDtypeStruct((rows, width), BF16)

    def blocks(lanes):
        return pltpu.VMEM((n_seq, own, lanes), BF16)

    full = pltpu.VMEM((rows, width), BF16)
    operands = (query_act, key_act, value_act, filter_taps, out_grad, out_weight, *tables)
    mixed, query_grad, u_grad, filter_grad = pl.pallas_call(
        functools.partial(layer_kernel, n_seq, n_ch),
        out_shape=(bf, bf, *[jax.ShapeDtypeStruct((n_seq, own, rows), BF16)] * 2),
        in_specs=[fixed] * 12,
        out_specs=(vmem,) * 4,
        scratch_shapes=[
            full,
            full,
            full,
            full,
            full,
            pltpu.VMEM(out_weight.shape, BF16),
            *[pltpu.VMEM(t.shape, t.dtype) for t in tables],
            blocks(2 * rows),
            blocks(2 * rows),
            blocks(rows),
            blocks(rows),
            blocks(rows),
            blocks(rows),
            blocks(rows),
            blocks(rows),
            pltpu.VMEM((n_ch, rows, width), BF16),
            pltpu.VMEM((len(SCATTER_MOVES), rows, width), BF16),
            pltpu.VMEM((len(SCATTER_MOVES), rows, width), BF16),
            pltpu.VMEM((2 * half, 2 * rows), F32),
            pltpu.VMEM((2, half, 2 * rows), F32),
            pltpu.VMEM((2, half, 2 * rows), BF16),
            pltpu.VMEM((2 * half, 2 * rows), BF16),
            pltpu.VMEM((width, rows), F32),
            pltpu.VMEM((width, rows), BF16),
            pltpu.SemaphoreType.DMA((12,)),
            pltpu.SemaphoreType.DMA((5,)),
            pltpu.SemaphoreType.DMA((5,)),
            pltpu.SemaphoreType.DMA((len(GATHER_MOVES),)),
            pltpu.SemaphoreType.DMA((len(GATHER_MOVES),)),
            pltpu.SemaphoreType.DMA((len(SCATTER_MOVES),)),
            pltpu.SemaphoreType.DMA((len(SCATTER_MOVES),)),
        ],
        compiler_params=pltpu.CompilerParams(
            collective_id=0, has_side_effects=True, vmem_limit_bytes=32 * 1024 * 1024
        ),
    )(*[pltpu.with_memory_space_constraint(a, pltpu.HBM) for a in operands])
    return pl.pallas_call(
        finish_kernel,
        out_shape=(bf, bf, bf, bf, jax.ShapeDtypeStruct((rows, width), F32)),
        in_specs=[vmem, vmem, vmem, vmem, fixed, fixed],
        out_specs=(fixed,) * 5,
        scratch_shapes=[full] * 4 + [pltpu.VMEM((rows, width), F32), pltpu.SemaphoreType.DMA((7,))],
        compiler_params=pltpu.CompilerParams(vmem_limit_bytes=32 * 1024 * 1024),
    )(mixed, query_grad, u_grad, filter_grad, key_act, value_act)


def solution(mesh):
    return jax.shard_map(
        per_device,
        mesh=mesh,
        in_specs=(P("seq", "ch"),) * 5 + (P("ch", None),),
        out_specs=(P("seq", "ch"),) * 5,
        check_vma=False,
    )
```
